1024 devices in a mesh: section: 16 (over z), expert: 64 (over x, y, core).
Axes of the slice: x: 4, y: 8, z: 16, core: 2. Of those that a mesh axis runs over, the one named last changes fastest.
Arguments:
- route_ids: int32 [1, 131072, 1], P(None, ('section', 'expert')), may hold values from 0 to 7; in each aligned block of 128 rows (0 to 127, 128 to 255, ..., all dimensions but the last counted through in order) at most 18 rows name the same one
- gate_pre: bfloat16 [16, 1, 64, 1152, 128], P('section', None, 'expert'), may hold values from -6 to 6
- up_pre: bfloat16 [16, 1, 64, 1152, 128], P('section', None, 'expert'), may hold values from -6 to 6
- hid_grad: bfloat16 [16, 1, 64, 1152, 128], P('section', None, 'expert'), may hold values from -6 to 6
- w_gate: bfloat16 [16, 64, 448, 1024], P('section', 'expert'), may hold values from -0.1875 to 0.1875
- w_up: bfloat16 [16, 64, 448, 1024], P('section', 'expert'), may hold values from -0.1875 to 0.1875
Outputs:
- to_previous: bfloat16 [1, 131072, 3584], P(None, ('section', 'expert'))
The draws below stay inside these ranges and needn't reach their ends.
Inputs may be any that keep to these rules, and one draw needn't show every extreme that they name: `route_ids`: in each micro-batch, no expert is named by more than 18 routes of one device's tokens, a bound that some block reaches of them; a token's routes name different experts.
All inputs are finite; a program needn't handle non-finite values.
Results may differ from the reference program's by a relative error of at most 0.0049.
Values may be sent and summed in bfloat16 or wider, within the bound.
A program may use at most 32 MiB of HBM per device.

```python
import math
import jax
import jax.numpy as jnp
import numpy as np
from jax import lax

D = 3584
FF = 1024
GRP = 8
TOPK = 1
MB = 1
TOK_MB = 128
EXPERTS = 8
CAP = 18
SLOTS = 1152
HQ = 128
DQ = 448
ROWS = 131072
N_SECTION = 16
N_EXPERT = 64


def levels(rng, shape, pieces, low, high):
    level = 1.0
    for dim, blocks in pieces:
        draws = jax.random.uniform(jax.random.fold_in(jax.random.fold_in(rng, 6), dim), (blocks,), jnp.float32, low / len(pieces), high / len(pieces))
        level = level * jnp.repeat(jnp.exp(draws), shape[dim] // blocks).reshape((-1,) + (1,) * (len(shape) - 1 - dim))
    return level


def deal_out(own_key, own, number, rows, number_of, top, most, slope):
    sequence = jax.random.permutation(own_key, number_of)
    crowded, common = shares(number_of, rows * top, most, slope, True), shares(number_of, rows * top, most, slope, False)
    places = jnp.arange(number_of)

    def named(tallies, rotation):
        used = int((tallies > 0).sum())
        fixed = max(1, used // 4)
        passed = fixed + (places - fixed + rotation * (used - fixed)) % max(1, number_of - fixed)
        return jnp.zeros((number_of,), jnp.int32).at[sequence[jnp.where(places < fixed, places, passed)]].set(jnp.asarray(tallies, jnp.int32))

    tallies = jnp.where(number % 4 == 0, named(crowded, number // 4), named(common, number - number // 4 - 1))
    mixed = jax.random.permutation(jax.random.fold_in(own, 3), number_of)
    source_of, taker = mixed[0:number_of // 2 * 2:2], mixed[1:number_of // 2 * 2:2]
    slack = jnp.minimum(tallies[source_of] - 1, most - tallies[taker]) // 2
    slack = jnp.where((source_of == sequence[0]) | (taker == sequence[0]) | (tallies[taker] == 0), 0, jnp.maximum(slack, 0))
    passed = jax.random.randint(jax.random.fold_in(own, 4), (number_of // 2,), 0, 1 << 20) % (slack + 1)
    tallies = tallies.at[source_of].add(-passed).at[taker].add(passed)
    members = jnp.searchsorted(jnp.cumsum(tallies), jnp.arange(rows * top), side="right").astype(jnp.int32)
    table = members.reshape(top, rows).T
    table = table[jax.random.permutation(jax.random.fold_in(own, 1), rows)]
    rotation = jax.random.randint(jax.random.fold_in(own, 2), (rows, 1), 0, top)
    return jnp.take_along_axis(table, (jnp.arange(top)[None, :] + rotation) % top, axis=1)


def shares(number_of, total, most, skew, full):
    weights = [(1 << 20) // math.isqrt(standing ** skew) + 1 for standing in range(1, number_of + 1)]
    largest = most if full else min(most, max(-(-total // number_of), total * weights[0] // sum(weights)))
    least = 1 if total - largest >= number_of - 1 else 0
    given, rest = [largest] + [least] * (number_of - 1), total - largest - least * (number_of - 1)
    while rest > 0:
        candidates = [i for i in range(1, number_of) if given[i] < largest] or [i for i in range(1, number_of) if given[i] < most]
        whole, remaining = sum([weights[i] for i in candidates]), rest
        for i in candidates:
            addition = min(most - given[i], max(1, remaining * weights[i] // whole), rest)
            given[i] = given[i] + addition
            rest = rest - addition
    return np.array(given)


def scatter_about(own_key, extent, spread, limit, cuts=(), held_as=jnp.bfloat16):
    array = jax.random.normal(own_key, extent, jnp.float32) * spread
    if len(cuts) > 0:
        array = levels(own_key, extent, cuts, -0.22, 0.18) * array
    return jnp.clip(array, min=-limit, max=limit).astype(held_as)


def setup_inputs(seed: int = 0) -> dict:
    key_of = jax.random.split(jax.random.key(seed), 7)
    route_ids_keys = jax.random.split(jax.random.fold_in(key_of[0], 1), MB * ROWS // TOK_MB)
    route_ids_turns = jax.random.permutation(jax.random.fold_in(key_of[0], 3), MB * ROWS // TOK_MB)
    route_ids = jax.vmap(lambda own, number: deal_out(jax.random.fold_in(key_of[0], 2), own, number, TOK_MB, EXPERTS, TOPK, CAP, 2))(route_ids_keys, route_ids_turns).reshape((MB, ROWS, TOPK))
    gate_pre = scatter_about(key_of[1], (N_SECTION, MB, N_EXPERT, SLOTS, HQ), 1.0, 6.0, ((0, 16), (2, 64)))
    up_pre = scatter_about(key_of[2], (N_SECTION, MB, N_EXPERT, SLOTS, HQ), 1.0, 6.0, ((0, 16), (2, 64)))
    hid_grad = scatter_about(key_of[3], (N_SECTION, MB, N_EXPERT, SLOTS, HQ), 1.0, 6.0, ((0, 16), (2, 64)))
    w_gate = scatter_about(key_of[4], (N_SECTION, N_EXPERT, DQ, FF), FF ** -0.5, 0.1875, ((0, 16), (1, 64)))
    w_up = scatter_about(key_of[5], (N_SECTION, N_EXPERT, DQ, FF), FF ** -0.5, 0.1875, ((0, 16), (1, 64)))
    return {"route_ids": route_ids, "gate_pre": gate_pre, "up_pre": up_pre, "hid_grad": hid_grad, "w_gate": w_gate, "w_up": w_up}


def derivatives(gate_part, up_part, grad_part):
    gate_val = gate_part.astype(jnp.float32)
    up_val = up_part.astype(jnp.float32)
    grad_val = grad_part.astype(jnp.float32)
    sigma = jax.nn.sigmoid(gate_val)
    gate_grad = (grad_val * up_val * sigma * (1.0 + gate_val * (1.0 - sigma))).astype(jnp.bfloat16)
    up_grad = (grad_val * gate_val * sigma).astype(jnp.bfloat16)
    return gate_grad, up_grad


def widen(part):
    shaped = part.reshape(MB, EXPERTS, GRP, SLOTS, HQ).transpose(0, 1, 3, 2, 4)
    return shaped.reshape(MB, EXPERTS, SLOTS, FF).astype(jnp.float32)


def section_rows(section, route_ids, gate_pre, up_pre, hid_grad, w_gate, w_up):
    gate_grad, up_grad = derivatives(gate_pre[section], up_pre[section], hid_grad[section])
    gate_mat = w_gate[section].reshape(EXPERTS, D, FF).astype(jnp.float32)
    up_mat = w_up[section].reshape(EXPERTS, D, FF).astype(jnp.float32)
    summed = jnp.einsum("mesf,edf->mesd", widen(gate_grad), gate_mat)
    summed = summed + jnp.einsum("mesf,edf->mesd", widen(up_grad), up_mat)
    slot_grad = summed.astype(jnp.bfloat16)
    routes = lax.dynamic_slice_in_dim(route_ids, section * (N_EXPERT * TOK_MB), N_EXPERT * TOK_MB, axis=1)
    routes = routes.reshape(MB, N_EXPERT, TOK_MB * TOPK).astype(jnp.int32)
    onehot = (routes[..., None] == jnp.arange(EXPERTS, dtype=jnp.int32)[None, None, None, :]).astype(jnp.int32)
    earlier = jnp.cumsum(onehot, axis=2) - onehot
    slot_pos = jnp.sum(onehot * earlier, axis=3).astype(jnp.int32)
    source = jnp.arange(N_EXPERT, dtype=jnp.int32)[None, :, None]
    flat_index = (routes * SLOTS + source * CAP + slot_pos).reshape(MB, -1).astype(jnp.int32)
    table = slot_grad.reshape(MB, EXPERTS * SLOTS, D)
    batch_index = jnp.arange(MB, dtype=jnp.int32)[:, None]
    picked = table[batch_index, flat_index]
    total = picked.reshape(MB, N_EXPERT * TOK_MB, TOPK, D).astype(jnp.float32).sum(axis=2)
    return total.astype(jnp.bfloat16)


def reference(route_ids, gate_pre, up_pre, hid_grad, w_gate, w_up):
    def one_section(section):
        return section_rows(section, route_ids, gate_pre, up_pre, hid_grad, w_gate, w_up)

    per_section = lax.map(one_section, jnp.arange(N_SECTION, dtype=jnp.int32))
    shifted = jnp.concatenate([per_section[1:], jnp.zeros_like(per_section[:1])], axis=0)
    return shifted.transpose(1, 0, 2, 3).reshape(MB, ROWS, D)
```

```python
import functools

import jax
import jax.numpy as jnp
from jax import lax
from jax.experimental import pallas as pl
from jax.experimental.pallas import tpu as pltpu
from jax.sharding import PartitionSpec as P

GRP = 8
CHIPS = 4
ROUNDS = 4
LANES = 128
MESH = pl.DeviceIdType.MESH


def kernel(
    sections, devices, cap,
    ids_ref, gate_ref, up_ref, hid_ref, wg_ref, wu_ref,
    out_ref,
    act, other, weight, acc, stage, msg, recv, ids_in, pick,
    act_recv, own_send, fwd_send, w_send, w_recv, w_local, id_send, id_recv, msg_send, msg_recv,
):
    experts = devices // GRP
    half = devices // 2
    per_round = half // ROUNDS
    rows = per_round * cap
    half_rows = half * cap
    feats = wg_ref.shape[0]
    blocks = 2 * feats // LANES

    s = lax.axis_index("section")
    p = lax.axis_index("expert")
    e = p // GRP
    c = (p % GRP) // 2
    k = p % 2
    turn = e % ROUNDS

    def near(chip, core):
        return (s, e * GRP + chip * 2 + core)

    has_left, has_right = c > 0, c < CHIPS - 1
    sends_back, gets_back = s > 0, s < sections - 1

    barrier = pltpu.get_barrier_semaphore()

    def greet(device):
        pl.semaphore_signal(barrier, inc=1, device_id=device, device_id_type=MESH)

    greet(near(c, 1 - k))

    @pl.when(has_left)
    def _():
        greet(near(c - 1, 0))
        greet(near(c - 1, 1))

    @pl.when(has_right)
    def _():
        greet(near(c + 1, 0))
        greet(near(c + 1, 1))

    @pl.when(gets_back)
    def _():
        greet((s + 1, p))
        owner_half = p // half

        def step(i, carry):
            greet((s + 1, 2 * i + owner_half))
            return carry

        lax.fori_loop(0, devices // 2, step, 0)

    w_rows = pl.ds(pl.multiple_of(k * feats, feats), feats)
    local_g = pltpu.make_async_copy(wg_ref, weight.at[0, w_rows], w_local.at[0])
    local_u = pltpu.make_async_copy(wu_ref, weight.at[1, w_rows], w_local.at[1])
    local_g.start()
    local_u.start()

    def derive(start):
        at = pl.ds(pl.multiple_of(start, 16), rows)
        gate_val = gate_ref[at, :].astype(jnp.float32)
        up_val = up_ref[at, :].astype(jnp.float32)
        grad_val = hid_ref[at, :].astype(jnp.float32)
        sigma = jax.nn.sigmoid(gate_val)
        part = grad_val * sigma
        gate_grad = part * up_val * (1.0 + gate_val * (1.0 - sigma))
        return gate_grad.astype(jnp.bfloat16), (part * gate_val).astype(jnp.bfloat16)

    def derive_round(r, carry):
        chunk = (r + turn) % ROUNDS
        gate_grad, up_grad = derive(k * half_rows + chunk * rows)
        act[c, r, k, :, :LANES] = gate_grad
        act[c, r, k, :, LANES:] = up_grad
        gate_grad, up_grad = derive((1 - k) * half_rows + chunk * rows)
        other[r, :, :LANES] = gate_grad
        other[r, :, LANES:] = up_grad
        return carry

    lax.fori_loop(0, ROUNDS, derive_round, 0)

    pl.semaphore_wait(
        barrier,
        1
        + 2 * has_left.astype(jnp.int32)
        + 2 * has_right.astype(jnp.int32)
        + (devices // 2 + 1) * sends_back.astype(jnp.int32),
    )

    def remote(src, dst, send, recv_sem, device):
        return pltpu.make_async_remote_copy(
            src_ref=src, dst_ref=dst, send_sem=send, recv_sem=recv_sem,
            device_id=device, device_id_type=MESH,
        )

    def own_copies(r, chip, side):
        same = remote(
            act.at[c, r, k], act.at[c, r, k], own_send.at[r, 2 * side], act_recv.at[c, r, k], near(chip, k)
        )
        cross = remote(
            other.at[r], act.at[c, r, k], own_send.at[r, 2 * side + 1], act_recv.at[c, r, k], near(chip, 1 - k)
        )
        return same, cross

    def own_partner(r):
        return remote(
            other.at[r], act.at[c, r, k], own_send.at[r, 4], act_recv.at[c, r, k], near(c, 1 - k)
        )

    def forward(r, source, chip, slot):
        return remote(
            act.at[source, r], act.at[source, r], fwd_send.at[r, slot], act_recv.at[source, r, 0], near(chip, k)
        )

    def each_own(r, what):
        @pl.when(has_left)
        def _():
            for copy in own_copies(r, c - 1, 0):
                what(copy)

        @pl.when(has_right)
        def _():
            for copy in own_copies(r, c + 1, 1):
                what(copy)

        what(own_partner(r))

    def arrived(ref, sem):
        pltpu.make_async_copy(ref, ref, sem).wait()

    weight_g = remote(wg_ref, weight.at[0, w_rows], w_send.at[0], w_recv.at[0], near(c, 1 - k))
    weight_u = remote(wu_ref, weight.at[1, w_rows], w_send.at[1], w_recv.at[1], near(c, 1 - k))
    id_copy = remote(ids_ref, ids_in, id_send.at[0], id_recv.at[0], (s - 1, p))

    each_own(0, lambda copy: copy.start())
    weight_g.start()
    weight_u.start()

    @pl.when(sends_back)
    def _():
        id_copy.start()

    stage[...] = jnp.zeros_like(stage)

    def back(r, i):
        owner = k * half + ((r + turn) % ROUNDS) * per_round + i
        return remote(
            msg.at[r, i], recv.at[c, e], msg_send.at[r, i], msg_recv.at[c, e], (s - 1, owner)
        )

    def round_step(r, carry):
        @pl.when(r + 1 < ROUNDS)
        def _():
            each_own(r + 1, lambda copy: copy.start())

        @pl.when(has_left)
        def _():
            arrived(act.at[c - 1, r, 0], act_recv.at[c - 1, r, 0])
            arrived(act.at[c - 1, r, 1], act_recv.at[c - 1, r, 1])

            @pl.when(has_right)
            def _():
                forward(r, c - 1, c + 1, 0).start()

        @pl.when(has_right)
        def _():
            arrived(act.at[c + 1, r, 0], act_recv.at[c + 1, r, 0])
            arrived(act.at[c + 1, r, 1], act_recv.at[c + 1, r, 1])

            @pl.when(has_left)
            def _():
                forward(r, c + 1, c - 1, 1).start()

        @pl.when(c >= 2)
        def _():
            arrived(act.at[c - 2, r], act_recv.at[c - 2, r, 0])

            @pl.when(has_right)
            def _():
                forward(r, c - 2, c + 1, 2).start()

        @pl.when(c < CHIPS - 2)
        def _():
            arrived(act.at[c + 2, r], act_recv.at[c + 2, r, 0])

            @pl.when(has_left)
            def _():
                forward(r, c + 2, c - 1, 3).start()

        arrived(act.at[c, r, 1 - k], act_recv.at[c, r, 1 - k])

        @pl.when(r == 0)
        def _():
            local_g.wait()
            local_u.wait()
            partner_rows = pl.ds(pl.multiple_of((1 - k) * feats, feats), feats)
            arrived(weight.at[0, partner_rows], w_recv.at[0])
            arrived(weight.at[1, partner_rows], w_recv.at[1])

        @pl.when(c == CHIPS - 1)
        def _():
            arrived(act.at[0, r], act_recv.at[0, r, 0])

        @pl.when(c == 0)
        def _():
            arrived(act.at[CHIPS - 1, r], act_recv.at[CHIPS - 1, r, 0])

        lhs = [
            jnp.concatenate(
                [act[chip, r, core, :, g * LANES:(g + 1) * LANES] for chip in range(CHIPS) for core in range(2)],
                axis=1,
            )
            for g in range(2)
        ]
        contract = (((1,), (1,)), ((), ()))
        for start in range(0, 2 * feats, 2 * LANES):
            size = min(2 * LANES, 2 * feats - start)
            total = None
            for g in range(2):
                term = lax.dot_general(
                    lhs[g], weight[g, start:start + size, :], contract, preferred_element_type=jnp.float32
                )
                total = term if total is None else total + term
            acc[:, start:start + size] = total

        for i in range(per_round):
            for n in range(blocks):
                stage[i % 2, n * cap:(n + 1) * cap, :] = acc[i * cap:(i + 1) * cap, n * LANES:(n + 1) * LANES]
            msg[r, i] = stage[i % 2].astype(jnp.bfloat16)

        @pl.when(sends_back)
        def _():
            def send(i, carry):
                back(r, (i + 2 * c + e) % per_round).start()
                return carry

            lax.fori_loop(0, per_round, send, 0)

        return carry

    lax.fori_loop(0, ROUNDS, round_step, 0)

    deep = recv.shape[2]
    width = experts * deep
    tokens = ids_ref.shape[1]

    @pl.when(gets_back)
    def _():
        arrived(ids_in, id_recv.at[0])
        row = jnp.broadcast_to(ids_in[...], (tokens, tokens))
        ti = lax.broadcasted_iota(jnp.int32, (tokens, tokens), 0)
        tj = lax.broadcasted_iota(jnp.int32, (tokens, tokens), 1)
        expert = jnp.sum(jnp.where(ti == tj, row, 0), axis=1, keepdims=True)
        earlier = jnp.where((row == expert) & (tj < ti), 1, 0)
        place = jnp.sum(earlier, axis=1, keepdims=True) + expert * deep
        lane = lax.broadcasted_iota(jnp.int32, (tokens, width), 1) - place
        for n in range(blocks):
            pick[n * tokens:(n + 1) * tokens, :] = jnp.where(lane == n * cap, 1.0, 0.0).astype(jnp.bfloat16)

        for chip in range(CHIPS):
            for expert_at in range(experts):
                arrived(recv.at[chip, expert_at], msg_recv.at[chip, expert_at])

        for pair in range(0, CHIPS, 2):
            rhs = jnp.concatenate(
                [recv[pair].reshape(width, LANES), recv[pair + 1].reshape(width, LANES)], axis=1
            )
            got = jnp.dot(pick[...], rhs, preferred_element_type=jnp.float32).astype(jnp.bfloat16)
            for j in range(2):
                for n in range(blocks):
                    at = ((pair + j) * blocks + n) * LANES
                    out_ref[:, at:at + LANES] = got[n * tokens:(n + 1) * tokens, j * LANES:(j + 1) * LANES]

    @pl.when(jnp.logical_not(gets_back))
    def _():
        out_ref[...] = jnp.zeros_like(out_ref)

    weight_g.wait_send()
    weight_u.wait_send()

    @pl.when(sends_back)
    def _():
        id_copy.wait_send()

    def drain(r, carry):
        each_own(r, lambda copy: copy.wait_send())

        @pl.when(has_left & has_right)
        def _():
            forward(r, c - 1, c + 1, 0).wait_send()
            forward(r, c + 1, c - 1, 1).wait_send()

        @pl.when((c >= 2) & has_right)
        def _():
            forward(r, c - 2, c + 1, 2).wait_send()

        @pl.when((c < CHIPS - 2) & has_left)
        def _():
            forward(r, c + 2, c - 1, 3).wait_send()

        @pl.when(sends_back)
        def _():
            def done(i, carry):
                back(r, i).wait_send()
                return carry

            lax.fori_loop(0, per_round, done, 0)

        return carry

    lax.fori_loop(0, ROUNDS, drain, 0)


def local(route_ids, gate_pre, up_pre, hid_grad, w_gate, w_up):
    sections, devices = lax.axis_size("section"), lax.axis_size("expert")
    slots, hidden = gate_pre.shape[3:]
    cap = slots // devices
    feats, width = w_gate.shape[2:]
    tokens = route_ids.shape[1]
    experts = devices // GRP
    per_round = devices // 2 // ROUNDS
    rows = per_round * cap
    blocks = 2 * feats // LANES
    deep = -(-blocks * cap // 16) * 16
    vmem = pl.BlockSpec(memory_space=pltpu.VMEM)
    hbm = pl.BlockSpec(memory_space=pl.ANY)
    bf16 = jnp.bfloat16
    dma = pltpu.SemaphoreType.DMA
    out = pl.pallas_call(
        functools.partial(kernel, sections, devices, cap),
        out_shape=jax.ShapeDtypeStruct((tokens, GRP * feats), bf16),
        in_specs=[vmem, vmem, vmem, vmem, hbm, hbm],
        out_specs=vmem,
        scratch_shapes=[
            pltpu.VMEM((CHIPS, ROUNDS, 2, rows, 2 * hidden), bf16),
            pltpu.VMEM((ROUNDS, rows, 2 * hidden), bf16),
            pltpu.VMEM((2, 2 * feats, width), bf16),
            pltpu.VMEM((rows, 2 * feats), jnp.float32),
            pltpu.VMEM((2, deep, LANES), jnp.float32),
            pltpu.VMEM((ROUNDS, per_round, deep, LANES), bf16),
            pltpu.VMEM((CHIPS, experts, deep, LANES), bf16),
            pltpu.VMEM((1, tokens), jnp.int32),
            pltpu.VMEM((blocks * tokens, experts * deep), bf16),
            dma((CHIPS, ROUNDS, 2)),
            dma((ROUNDS, 5)),
            dma((ROUNDS, 4)),
            dma((2,)),
            dma((2,)),
            dma((2,)),
            dma((1,)),
            dma((1,)),
            dma((ROUNDS, per_round)),
            dma((CHIPS, experts)),
        ],
        compiler_params=pltpu.CompilerParams(
            collective_id=0, has_side_effects=True, vmem_limit_bytes=48 * 1024 * 1024
        ),
        name="moe_input_grad",
    )(
        route_ids.reshape(1, tokens),
        gate_pre[0, 0, 0],
        up_pre[0, 0, 0],
        hid_grad[0, 0, 0],
        w_gate[0, 0],
        w_up[0, 0],
    )
    return out[None]


def solution(mesh):
    placed = (
        P(None, ("section", "expert"), None),
        P("section", None, "expert", None, None),
        P("section", None, "expert", None, None),
        P("section", None, "expert", None, None),
        P("section", "expert", None, None),
        P("section", "expert", None, None),
    )
    return jax.shard_map(
        local,
        mesh=mesh,
        in_specs=placed,
        out_specs=P(None, ("section", "expert"), None),
        check_vma=False,
    )
```

```python
import functools

import jax
import jax.numpy as jnp
from jax import lax
from jax.experimental import pallas as pl
from jax.experimental.pallas import tpu as pltpu
from jax.sharding import PartitionSpec as P

GRP = 8
CHIPS = 4
ROUNDS = 4
GRID_X, GRID_Y = 4, 8
SPREAD = GRID_X // 2 + GRID_Y // 2 + 1
LANES = 128
MESH = pl.DeviceIdType.MESH


def kernel(
    sections, devices, cap,
    ids_ref, gate_ref, up_ref, hid_ref, wg_ref, wu_ref,
    out_ref,
    gate_in, up_in, hid_in, act, other, weight, acc, stage, msg, recv, ids_in, pick,
    act_recv, own_send, fwd_send, w_send, w_recv, w_local, in_local, id_send, id_recv, msg_send, msg_recv, told,
):
    experts = devices // GRP
    half = devices // 2
    per_round = half // ROUNDS
    rows = per_round * cap
    half_rows = half * cap
    feats = wg_ref.shape[0]
    blocks = 2 * feats // LANES

    s = lax.axis_index("section")
    p = lax.axis_index("expert")
    e = p // GRP
    c = (p % GRP) // 2
    k = p % 2
    turn = e % ROUNDS

    def near(chip, core):
        return (s, e * GRP + chip * 2 + core)

    has_left, has_right = c > 0, c < CHIPS - 1
    sends_back, gets_back = s > 0, s < sections - 1
    x, y = p // (2 * GRID_Y), p // 2 % GRID_Y

    def at_grid(gx, gy):
        return (s, ((gx + GRID_X) % GRID_X * GRID_Y + (gy + GRID_Y) % GRID_Y) * 2 + k)

    barrier = pltpu.get_barrier_semaphore()

    def greet(device):
        pl.semaphore_signal(barrier, inc=1, device_id=device, device_id_type=MESH)

    @pl.when(gets_back)
    def _():
        greet((s + 1, p))

    @pl.when(sends_back)
    def _():
        greet(near(c, 1 - k))
        for gx, gy in ((x - 1, y), (x + 1, y), (x, y - 1), (x, y + 1)):
            greet(at_grid(gx, gy))

        @pl.when(has_left)
        def _():
            greet(near(c - 1, 1 - k))

        @pl.when(has_right)
        def _():
            greet(near(c + 1, 1 - k))

    def tell(step):
        if step < GRID_X // 2:
            devices_told = [at_grid(x - 1, y), at_grid(x + 1, y)]
        elif step < SPREAD - 1:
            devices_told = [at_grid(x, y - 1), at_grid(x, y + 1)]
        else:
            devices_told = [near(c, 1 - k)]
        for device in devices_told:
            pl.semaphore_signal(told.at[step], inc=1, device_id=device, device_id_type=MESH)

    def hear(step):
        pl.semaphore_wait(told.at[step], 1 if step == SPREAD - 1 else 2)

    w_rows = pl.ds(pl.multiple_of(k * feats, feats), feats)
    local_g = pltpu.make_async_copy(wg_ref, weight.at[0, w_rows], w_local.at[0])
    local_u = pltpu.make_async_copy(wu_ref, weight.at[1, w_rows], w_local.at[1])
    loads = [
        pltpu.make_async_copy(ref, dst, in_local.at[i])
        for i, (ref, dst) in enumerate(((gate_ref, gate_in), (up_ref, up_in), (hid_ref, hid_in)))
    ]

    def derive(start):
        at = pl.ds(pl.multiple_of(start, 16), rows)
        gate_val = gate_in[at, :].astype(jnp.float32)
        up_val = up_in[at, :].astype(jnp.float32)
        grad_val = hid_in[at, :].astype(jnp.float32)
        sigma = jax.nn.sigmoid(gate_val)
        part = grad_val * sigma
        gate_grad = part * up_val * (1.0 + gate_val * (1.0 - sigma))
        return gate_grad.astype(jnp.bfloat16), (part * gate_val).astype(jnp.bfloat16)

    def derive_round(r):
        chunk = (r + turn) % ROUNDS
        gate_grad, up_grad = derive(k * half_rows + chunk * rows)
        act[c, r, k, :, :LANES] = gate_grad
        act[c, r, k, :, LANES:] = up_grad
        gate_grad, up_grad = derive((1 - k) * half_rows + chunk * rows)
        other[r, :, :LANES] = gate_grad
        other[r, :, LANES:] = up_grad

    def remote(src, dst, send, recv_sem, device):
        return pltpu.make_async_remote_copy(
            src_ref=src, dst_ref=dst, send_sem=send, recv_sem=recv_sem,
            device_id=device, device_id_type=MESH,
        )

    def own_copies(r, chip, side):
        same = remote(
            act.at[c, r, k], act.at[c, r, k], own_send.at[r, 2 * side], act_recv.at[c, r, k], near(chip, k)
        )
        cross = remote(
            other.at[r], act.at[c, r, k], own_send.at[r, 2 * side + 1], act_recv.at[c, r, k], near(chip, 1 - k)
        )
        return same, cross

    def own_partner(r):
        return remote(
            other.at[r], act.at[c, r, k], own_send.at[r, 4], act_recv.at[c, r, k], near(c, 1 - k)
        )

    def forward(r, source, chip, slot):
        return remote(
            act.at[source, r], act.at[source, r], fwd_send.at[r, slot], act_recv.at[source, r, 0], near(chip, k)
        )

    def each_own(r, what):
        @pl.when(has_left)
        def _():
            for copy in own_copies(r, c - 1, 0):
                what(copy)

        @pl.when(has_right)
        def _():
            for copy in own_copies(r, c + 1, 1):
                what(copy)

        what(own_partner(r))

    def arrived(ref, sem):
        pltpu.make_async_copy(ref, ref, sem).wait()

    weight_g = remote(wg_ref, weight.at[0, w_rows], w_send.at[0], w_recv.at[0], near(c, 1 - k))
    weight_u = remote(wu_ref, weight.at[1, w_rows], w_send.at[1], w_recv.at[1], near(c, 1 - k))
    id_copy = remote(ids_ref, ids_in, id_send.at[0], id_recv.at[0], (s - 1, p))

    @pl.when(sends_back)
    def _():
        for load in loads:
            load.start()
        local_g.start()
        local_u.start()
        for load in loads:
            load.wait()
        derive_round(0)
        pl.semaphore_wait(
            barrier, 6 + has_left.astype(jnp.int32) + has_right.astype(jnp.int32)
        )
        each_own(0, lambda copy: copy.start())
        weight_g.start()
        weight_u.start()
        id_copy.start()
        tell(0)

        def early(r, carry):
            derive_round(r)

            @pl.when(r == 1)
            def _():
                each_own(1, lambda copy: copy.start())

            return carry

        lax.fori_loop(1, ROUNDS, early, 0)
        stage[...] = jnp.zeros_like(stage)

    def back(r, i):
        owner = k * half + ((r + turn) % ROUNDS) * per_round + i
        return remote(
            msg.at[r, i], recv.at[c, e], msg_send.at[r, i], msg_recv.at[c, e], (s - 1, owner)
        )

    def relay(r):
        @pl.when((r > 0) & (r + 1 < ROUNDS))
        def _():
            each_own(r + 1, lambda copy: copy.start())

        @pl.when(has_left)
        def _():
            arrived(act.at[c - 1, r, 0], act_recv.at[c - 1, r, 0])
            arrived(act.at[c - 1, r, 1], act_recv.at[c - 1, r, 1])

            @pl.when(has_right)
            def _():
                forward(r, c - 1, c + 1, 0).start()

        @pl.when(has_right)
        def _():
            arrived(act.at[c + 1, r, 0], act_recv.at[c + 1, r, 0])
            arrived(act.at[c + 1, r, 1], act_recv.at[c + 1, r, 1])

            @pl.when(has_left)
            def _():
                forward(r, c + 1, c - 1, 1).start()

        for turn_of in range(2):
            @pl.when(r == turn_of)
            def _(step=2 * turn_of):
                hear(step)
                tell(step + 1)

        @pl.when(c >= 2)
        def _():
            arrived(act.at[c - 2, r], act_recv.at[c - 2, r, 0])

            @pl.when(has_right)
            def _():
                forward(r, c - 2, c + 1, 2).start()

        @pl.when(c < CHIPS - 2)
        def _():
            arrived(act.at[c + 2, r], act_recv.at[c + 2, r, 0])

            @pl.when(has_left)
            def _():
                forward(r, c + 2, c - 1, 3).start()

        for turn_of in range(2):
            @pl.when(r == turn_of)
            def _(step=2 * turn_of + 1):
                hear(step)
                tell(step + 1)

    def compute(r):
        arrived(act.at[c, r, 1 - k], act_recv.at[c, r, 1 - k])

        @pl.when(r == 0)
        def _():
            local_g.wait()
            local_u.wait()
            partner_rows = pl.ds(pl.multiple_of((1 - k) * feats, feats), feats)
            arrived(weight.at[0, partner_rows], w_recv.at[0])
            arrived(weight.at[1, partner_rows], w_recv.at[1])

        @pl.when(c == CHIPS - 1)
        def _():
            arrived(act.at[0, r], act_recv.at[0, r, 0])

        @pl.when(c == 0)
        def _():
            arrived(act.at[CHIPS - 1, r], act_recv.at[CHIPS - 1, r, 0])

        @pl.when(r == 0)
        def _():
            hear(4)
            tell(5)

        lhs = [
            jnp.concatenate(
                [act[chip, r, core, :, g * LANES:(g + 1) * LANES] for chip in range(CHIPS) for core in range(2)],
                axis=1,
            )
            for g in range(2)
        ]
        contract = (((1,), (1,)), ((), ()))
        for start in range(0, 2 * feats, 2 * LANES):
            size = min(2 * LANES, 2 * feats - start)
            total = None
            for g in range(2):
                term = lax.dot_general(
                    lhs[g], weight[g, start:start + size, :], contract, preferred_element_type=jnp.float32
                )
                total = term if total is None else total + term
            acc[:, start:start + size] = total

        @pl.when(r == 0)
        def _():
            hear(5)
            tell(6)

        for i in range(per_round):
            for n in range(blocks):
                stage[i % 2, n * cap:(n + 1) * cap, :] = acc[i * cap:(i + 1) * cap, n * LANES:(n + 1) * LANES]
            msg[r, i] = stage[i % 2].astype(jnp.bfloat16)

        @pl.when(r == 0)
        def _():
            hear(6)

        def send(i, carry):
            back(r, (i + 2 * c + e) % per_round).start()
            return carry

        lax.fori_loop(0, per_round, send, 0)

    def round_step(r, carry):
        @pl.when(r < ROUNDS)
        def _():
            relay(r)

        @pl.when(r > 0)
        def _():
            compute(r - 1)

        return carry

    @pl.when(sends_back)
    def _():
        lax.fori_loop(0, ROUNDS + 1, round_step, 0)

    deep = recv.shape[2]
    width = experts * deep
    tokens = ids_ref.shape[1]

    @pl.when(gets_back)
    def _():
        arrived(ids_in, id_recv.at[0])
        row = jnp.broadcast_to(ids_in[...], (tokens, tokens))
        ti = lax.broadcasted_iota(jnp.int32, (tokens, tokens), 0)
        tj = lax.broadcasted_iota(jnp.int32, (tokens, tokens), 1)
        expert = jnp.sum(jnp.where(ti == tj, row, 0), axis=1, keepdims=True)
        earlier = jnp.where((row == expert) & (tj < ti), 1, 0)
        place = jnp.sum(earlier, axis=1, keepdims=True) + expert * deep
        lane = lax.broadcasted_iota(jnp.int32, (tokens, width), 1) - place
        for n in range(blocks):
            pick[n * tokens:(n + 1) * tokens, :] = jnp.where(lane == n * cap, 1.0, 0.0).astype(jnp.bfloat16)

        for chip in range(CHIPS):
            for expert_at in range(experts):
                arrived(recv.at[chip, expert_at], msg_recv.at[chip, expert_at])

        for pair in range(0, CHIPS, 2):
            rhs = jnp.concatenate(
                [recv[pair].reshape(width, LANES), recv[pair + 1].reshape(width, LANES)], axis=1
            )
            got = jnp.dot(pick[...], rhs, preferred_element_type=jnp.float32).astype(jnp.bfloat16)
            for j in range(2):
                for n in range(blocks):
                    at = ((pair + j) * blocks + n) * LANES
                    out_ref[:, at:at + LANES] = got[n * tokens:(n + 1) * tokens, j * LANES:(j + 1) * LANES]

    @pl.when(jnp.logical_not(gets_back))
    def _():
        out_ref[...] = jnp.zeros_like(out_ref)

    def drain(r, carry):
        each_own(r, lambda copy: copy.wait_send())

        @pl.when(has_left & has_right)
        def _():
            forward(r, c - 1, c + 1, 0).wait_send()
            forward(r, c + 1, c - 1, 1).wait_send()

        @pl.when((c >= 2) & has_right)
        def _():
            forward(r, c - 2, c + 1, 2).wait_send()

        @pl.when((c < CHIPS - 2) & has_left)
        def _():
            forward(r, c + 2, c - 1, 3).wait_send()

        def done(i, carry):
            back(r, i).wait_send()
            return carry

        lax.fori_loop(0, per_round, done, 0)
        return carry

    @pl.when(sends_back)
    def _():
        weight_g.wait_send()
        weight_u.wait_send()
        id_copy.wait_send()
        lax.fori_loop(0, ROUNDS, drain, 0)


def local(route_ids, gate_pre, up_pre, hid_grad, w_gate, w_up):
    sections, devices = lax.axis_size("section"), lax.axis_size("expert")
    slots, hidden = gate_pre.shape[3:]
    cap = slots // devices
    feats, width = w_gate.shape[2:]
    tokens = route_ids.shape[1]
    experts = devices // GRP
    per_round = devices // 2 // ROUNDS
    rows = per_round * cap
    blocks = 2 * feats // LANES
    deep = -(-blocks * cap // 16) * 16
    vmem = pl.BlockSpec(memory_space=pltpu.VMEM)
    hbm = pl.BlockSpec(memory_space=pl.ANY)
    bf16 = jnp.bfloat16
    dma = pltpu.SemaphoreType.DMA
    out = pl.pallas_call(
        functools.partial(kernel, sections, devices, cap),
        out_shape=jax.ShapeDtypeStruct((tokens, GRP * feats), bf16),
        in_specs=[vmem, hbm, hbm, hbm, hbm, hbm],
        out_specs=vmem,
        scratch_shapes=[
            pltpu.VMEM((slots, hidden), bf16),
            pltpu.VMEM((slots, hidden), bf16),
            pltpu.VMEM((slots, hidden), bf16),
            pltpu.VMEM((CHIPS, ROUNDS, 2, rows, 2 * hidden), bf16),
            pltpu.VMEM((ROUNDS, rows, 2 * hidden), bf16),
            pltpu.VMEM((2, 2 * feats, width), bf16),
            pltpu.VMEM((rows, 2 * feats), jnp.float32),
            pltpu.VMEM((2, deep, LANES), jnp.float32),
            pltpu.VMEM((ROUNDS, per_round, deep, LANES), bf16),
            pltpu.VMEM((CHIPS, experts, deep, LANES), bf16),
            pltpu.VMEM((1, tokens), jnp.int32),
            pltpu.VMEM((blocks * tokens, experts * deep), bf16),
            dma((CHIPS, ROUNDS, 2)),
            dma((ROUNDS, 5)),
            dma((ROUNDS, 4)),
            dma((2,)),
            dma((2,)),
            dma((2,)),
            dma((3,)),
            dma((1,)),
            dma((1,)),
            dma((ROUNDS, per_round)),
            dma((CHIPS, experts)),
            pltpu.SemaphoreType.REGULAR((SPREAD,)),
        ],
        compiler_params=pltpu.CompilerParams(
            collective_id=0, has_side_effects=True, vmem_limit_bytes=67_043_328
        ),
        name="moe_input_grad",
    )(
        route_ids.reshape(1, tokens),
        gate_pre[0, 0, 0],
        up_pre[0, 0, 0],
        hid_grad[0, 0, 0],
        w_gate[0, 0],
        w_up[0, 0],
    )
    return out[None]


def solution(mesh):
    placed = (
        P(None, ("section", "expert"), None),
        P("section", None, "expert", None, None),
        P("section", None, "expert", None, None),
        P("section", None, "expert", None, None),
        P("section", "expert", None, None),
        P("section", "expert", None, None),
    )
    return jax.shard_map(
        local,
        mesh=mesh,
        in_specs=placed,
        out_specs=P(None, ("section", "expert"), None),
        check_vma=False,
    )
```

```python
import functools

import jax
import jax.numpy as jnp
from jax import lax
from jax.experimental import pallas as pl
from jax.experimental.pallas import tpu as pltpu
from jax.sharding import PartitionSpec as P

GRP = 8
CHIPS = 4
ROUNDS = 4
AHEAD = 4
GRID_X, GRID_Y = 4, 8
SPREAD = GRID_X // 2 + GRID_Y // 2 + 1
LANES = 128
MESH = pl.DeviceIdType.MESH


def kernel(
    sections, devices, cap,
    ids_ref, gate_ref, up_ref, hid_ref, wg_ref, wu_ref,
    out_ref,
    gate_in, up_in, hid_in, act, other, weight, acc, stage, msg, recv, ids_in, pick,
    act_recv, own_send, fwd_send, w_send, w_recv, w_local, in_local, id_send, id_recv, msg_send, msg_recv, told,
):
    experts = devices // GRP
    half = devices // 2
    per_round = half // ROUNDS
    rows = per_round * cap
    half_rows = half * cap
    feats = wg_ref.shape[0]
    blocks = 2 * feats // LANES

    s = lax.axis_index("section")
    p = lax.axis_index("expert")
    e = p // GRP
    c = (p % GRP) // 2
    k = p % 2
    turn = e % ROUNDS

    def near(chip, core):
        return (s, e * GRP + chip * 2 + core)

    has_left, has_right = c > 0, c < CHIPS - 1
    sends_back, gets_back = s > 0, s < sections - 1
    x, y = p // (2 * GRID_Y), p // 2 % GRID_Y

    def at_grid(gx, gy):
        return (s, ((gx + GRID_X) % GRID_X * GRID_Y + (gy + GRID_Y) % GRID_Y) * 2 + k)

    barrier = pltpu.get_barrier_semaphore()

    def greet(device):
        pl.semaphore_signal(barrier, inc=1, device_id=device, device_id_type=MESH)

    @pl.when(gets_back)
    def _():
        greet((s + 1, p))

    @pl.when(sends_back)
    def _():
        greet(near(c, 1 - k))
        for gx, gy in ((x - 1, y), (x + 1, y), (x, y - 1), (x, y + 1)):
            greet(at_grid(gx, gy))

        @pl.when(has_left)
        def _():
            greet(near(c - 1, 1 - k))

        @pl.when(has_right)
        def _():
            greet(near(c + 1, 1 - k))

    def tell(step):
        if step < GRID_X // 2:
            devices_told = [at_grid(x - 1, y), at_grid(x + 1, y)]
        elif step < SPREAD - 1:
            devices_told = [at_grid(x, y - 1), at_grid(x, y + 1)]
        else:
            devices_told = [near(c, 1 - k)]
        for device in devices_told:
            pl.semaphore_signal(told.at[step], inc=1, device_id=device, device_id_type=MESH)

    def hear(step):
        pl.semaphore_wait(told.at[step], 1 if step == SPREAD - 1 else 2)

    w_rows = pl.ds(pl.multiple_of(k * feats, feats), feats)
    local_g = pltpu.make_async_copy(wg_ref, weight.at[0, w_rows], w_local.at[0])
    local_u = pltpu.make_async_copy(wu_ref, weight.at[1, w_rows], w_local.at[1])
    loads = [
        pltpu.make_async_copy(ref, dst, in_local.at[i])
        for i, (ref, dst) in enumerate(((gate_ref, gate_in), (up_ref, up_in), (hid_ref, hid_in)))
    ]

    def derive(start):
        at = pl.ds(pl.multiple_of(start, 8), rows)
        gate_val = gate_in[at, :].astype(jnp.float32)
        up_val = up_in[at, :].astype(jnp.float32)
        grad_val = hid_in[at, :].astype(jnp.float32)
        sigma = jax.nn.sigmoid(gate_val)
        part = grad_val * sigma
        gate_grad = part * up_val * (1.0 + gate_val * (1.0 - sigma))
        return gate_grad.astype(jnp.bfloat16), (part * gate_val).astype(jnp.bfloat16)

    def derive_round(r):
        chunk = (r + turn) % ROUNDS
        gate_grad, up_grad = derive(k * half_rows + chunk * rows)
        act[c, r, k, :, :LANES] = gate_grad
        act[c, r, k, :, LANES:] = up_grad
        gate_grad, up_grad = derive((1 - k) * half_rows + chunk * rows)
        other[r, :, :LANES] = gate_grad
        other[r, :, LANES:] = up_grad

    def remote(src, dst, send, recv_sem, device):
        return pltpu.make_async_remote_copy(
            src_ref=src, dst_ref=dst, send_sem=send, recv_sem=recv_sem,
            device_id=device, device_id_type=MESH,
        )

    def own_copies(r, chip, side):
        same = remote(
            act.at[c, r, k], act.at[c, r, k], own_send.at[r, 2 * side], act_recv.at[c, r, k], near(chip, k)
        )
        cross = remote(
            other.at[r], act.at[c, r, k], own_send.at[r, 2 * side + 1], act_recv.at[c, r, k], near(chip, 1 - k)
        )
        return same, cross

    def own_partner(r):
        return remote(
            other.at[r], act.at[c, r, k], own_send.at[r, 4], act_recv.at[c, r, k], near(c, 1 - k)
        )

    def forward(r, source, chip, slot):
        return remote(
            act.at[source, r], act.at[source, r], fwd_send.at[r, slot], act_recv.at[source, r, 0], near(chip, k)
        )

    def each_own(r, what):
        @pl.when(has_left)
        def _():
            for copy in own_copies(r, c - 1, 0):
                what(copy)

        @pl.when(has_right)
        def _():
            for copy in own_copies(r, c + 1, 1):
                what(copy)

        what(own_partner(r))

    def arrived(ref, sem):
        pltpu.make_async_copy(ref, ref, sem).wait()

    weight_g = remote(wg_ref, weight.at[0, w_rows], w_send.at[0], w_recv.at[0], near(c, 1 - k))
    weight_u = remote(wu_ref, weight.at[1, w_rows], w_send.at[1], w_recv.at[1], near(c, 1 - k))
    id_copy = remote(ids_ref, ids_in, id_send.at[0], id_recv.at[0], (s - 1, p))

    @pl.when(sends_back)
    def _():
        for load in loads:
            load.start()
        local_g.start()
        local_u.start()
        for load in loads:
            load.wait()
        derive_round(0)
        pl.semaphore_wait(
            barrier, 6 + has_left.astype(jnp.int32) + has_right.astype(jnp.int32)
        )
        each_own(0, lambda copy: copy.start())
        weight_g.start()
        weight_u.start()
        id_copy.start()
        tell(0)

        def early(r, carry):
            derive_round(r)

            @pl.when(r < AHEAD)
            def _():
                each_own(r, lambda copy: copy.start())

            return carry

        lax.fori_loop(1, ROUNDS, early, 0)
        stage[...] = jnp.zeros_like(stage)

    def back(r, i):
        owner = k * half + ((r + turn) % ROUNDS) * per_round + i
        return remote(
            msg.at[r, i], recv.at[c, e], msg_send.at[r, i], msg_recv.at[c, e], (s - 1, owner)
        )

    def relay(r):
        @pl.when((r > 0) & (r + AHEAD - 1 < ROUNDS))
        def _():
            each_own(r + AHEAD - 1, lambda copy: copy.start())

        @pl.when(has_left)
        def _():
            arrived(act.at[c - 1, r, 0], act_recv.at[c - 1, r, 0])
            arrived(act.at[c - 1, r, 1], act_recv.at[c - 1, r, 1])

            @pl.when(has_right)
            def _():
                forward(r, c - 1, c + 1, 0).start()

        @pl.when(has_right)
        def _():
            arrived(act.at[c + 1, r, 0], act_recv.at[c + 1, r, 0])
            arrived(act.at[c + 1, r, 1], act_recv.at[c + 1, r, 1])

            @pl.when(has_left)
            def _():
                forward(r, c + 1, c - 1, 1).start()

        for turn_of in range(2):
            @pl.when(r == turn_of)
            def _(step=2 * turn_of):
                hear(step)
                tell(step + 1)

        @pl.when(c >= 2)
        def _():
            arrived(act.at[c - 2, r], act_recv.at[c - 2, r, 0])

            @pl.when(has_right)
            def _():
                forward(r, c - 2, c + 1, 2).start()

        @pl.when(c < CHIPS - 2)
        def _():
            arrived(act.at[c + 2, r], act_recv.at[c + 2, r, 0])

            @pl.when(has_left)
            def _():
                forward(r, c + 2, c - 1, 3).start()

        for turn_of in range(2):
            @pl.when(r == turn_of)
            def _(step=2 * turn_of + 1):
                hear(step)
                tell(step + 1)

    def compute(r):
        arrived(act.at[c, r, 1 - k], act_recv.at[c, r, 1 - k])

        @pl.when(r == 0)
        def _():
            local_g.wait()
            local_u.wait()
            partner_rows = pl.ds(pl.multiple_of((1 - k) * feats, feats), feats)
            arrived(weight.at[0, partner_rows], w_recv.at[0])
            arrived(weight.at[1, partner_rows], w_recv.at[1])

        @pl.when(c == CHIPS - 1)
        def _():
            arrived(act.at[0, r], act_recv.at[0, r, 0])

        @pl.when(c == 0)
        def _():
            arrived(act.at[CHIPS - 1, r], act_recv.at[CHIPS - 1, r, 0])

        @pl.when(r == 0)
        def _():
            hear(4)
            tell(5)

        lhs = [
            jnp.concatenate(
                [act[chip, r, core, :, g * LANES:(g + 1) * LANES] for chip in range(CHIPS) for core in range(2)],
                axis=1,
            )
            for g in range(2)
        ]
        contract = (((1,), (1,)), ((), ()))
        for start in range(0, 2 * feats, 2 * LANES):
            size = min(2 * LANES, 2 * feats - start)
            total = None
            for g in range(2):
                term = lax.dot_general(
                    lhs[g], weight[g, start:start + size, :], contract, preferred_element_type=jnp.float32
                )
                total = term if total is None else total + term
            acc[:, start:start + size] = total

        @pl.when(r == 0)
        def _():
            hear(5)
            tell(6)

        for i in range(per_round):
            for n in range(blocks):
                stage[i % 2, n * cap:(n + 1) * cap, :] = acc[i * cap:(i + 1) * cap, n * LANES:(n + 1) * LANES]
            msg[r, i] = stage[i % 2].astype(jnp.bfloat16)

        @pl.when(r == 0)
        def _():
            hear(6)

        def send(i, carry):
            back(r, (i + 2 * c + e) % per_round).start()
            return carry

        lax.fori_loop(0, per_round, send, 0)

    @pl.when(sends_back)
    def _():
        def relay_step(r, carry):
            relay(r)
            return carry

        def compute_step(r, carry):
            compute(r)
            return carry

        lax.fori_loop(0, ROUNDS, relay_step, 0)
        lax.fori_loop(0, ROUNDS, compute_step, 0)

    deep = recv.shape[2]
    width = experts * deep
    tokens = ids_ref.shape[1]

    @pl.when(gets_back)
    def _():
        arrived(ids_in, id_recv.at[0])
        row = jnp.broadcast_to(ids_in[...], (tokens, tokens))
        ti = lax.broadcasted_iota(jnp.int32, (tokens, tokens), 0)
        tj = lax.broadcasted_iota(jnp.int32, (tokens, tokens), 1)
        expert = jnp.sum(jnp.where(ti == tj, row, 0), axis=1, keepdims=True)
        earlier = jnp.where((row == expert) & (tj < ti), 1, 0)
        place = jnp.sum(earlier, axis=1, keepdims=True) + expert * deep
        lane = lax.broadcasted_iota(jnp.int32, (tokens, width), 1) - place
        for n in range(blocks):
            pick[n * tokens:(n + 1) * tokens, :] = jnp.where(lane == n * cap, 1.0, 0.0).astype(jnp.bfloat16)

        for pair in range(0, CHIPS, 2):
            for chip in (pair, pair + 1):
                for expert_at in range(experts):
                    arrived(recv.at[chip, expert_at], msg_recv.at[chip, expert_at])

            rhs = jnp.concatenate(
                [recv[pair].reshape(width, LANES), recv[pair + 1].reshape(width, LANES)], axis=1
            )
            got = jnp.dot(pick[...], rhs, preferred_element_type=jnp.float32).astype(jnp.bfloat16)
            for j in range(2):
                for n in range(blocks):
                    at = ((pair + j) * blocks + n) * LANES
                    out_ref[:, at:at + LANES] = got[n * tokens:(n + 1) * tokens, j * LANES:(j + 1) * LANES]

    @pl.when(jnp.logical_not(gets_back))
    def _():
        out_ref[...] = jnp.zeros_like(out_ref)

    def drain(r, carry):
        each_own(r, lambda copy: copy.wait_send())

        @pl.when(has_left & has_right)
        def _():
            forward(r, c - 1, c + 1, 0).wait_send()
            forward(r, c + 1, c - 1, 1).wait_send()

        @pl.when((c >= 2) & has_right)
        def _():
            forward(r, c - 2, c + 1, 2).wait_send()

        @pl.when((c < CHIPS - 2) & has_left)
        def _():
            forward(r, c + 2, c - 1, 3).wait_send()

        def done(i, carry):
            back(r, i).wait_send()
            return carry

        lax.fori_loop(0, per_round, done, 0)
        return carry

    @pl.when(sends_back)
    def _():
        weight_g.wait_send()
        weight_u.wait_send()
        id_copy.wait_send()
        lax.fori_loop(0, ROUNDS, drain, 0)


def local(route_ids, gate_pre, up_pre, hid_grad, w_gate, w_up):
    sections, devices = lax.axis_size("section"), lax.axis_size("expert")
    slots, hidden = gate_pre.shape[3:]
    cap = slots // devices
    feats, width = w_gate.shape[2:]
    tokens = route_ids.shape[1]
    experts = devices // GRP
    per_round = devices // 2 // ROUNDS
    rows = per_round * cap
    blocks = 2 * feats // LANES
    deep = -(-blocks * cap // 16) * 16
    vmem = pl.BlockSpec(memory_space=pltpu.VMEM)
    hbm = pl.BlockSpec(memory_space=pl.ANY)
    bf16 = jnp.bfloat16
    dma = pltpu.SemaphoreType.DMA
    out = pl.pallas_call(
        functools.partial(kernel, sections, devices, cap),
        out_shape=jax.ShapeDtypeStruct((tokens, GRP * feats), bf16),
        in_specs=[vmem, hbm, hbm, hbm, hbm, hbm],
        out_specs=vmem,
        scratch_shapes=[
            pltpu.VMEM((slots, hidden), bf16),
            pltpu.VMEM((slots, hidden), bf16),
            pltpu.VMEM((slots, hidden), bf16),
            pltpu.VMEM((CHIPS, ROUNDS, 2, rows, 2 * hidden), bf16),
            pltpu.VMEM((ROUNDS, rows, 2 * hidden), bf16),
            pltpu.VMEM((2, 2 * feats, width), bf16),
            pltpu.VMEM((rows, 2 * feats), jnp.float32),
            pltpu.VMEM((2, deep, LANES), jnp.float32),
            pltpu.VMEM((ROUNDS, per_round, deep, LANES), bf16),
            pltpu.VMEM((CHIPS, experts, deep, LANES), bf16),
            pltpu.VMEM((1, tokens), jnp.int32),
            pltpu.VMEM((blocks * tokens, experts * deep), bf16),
            dma((CHIPS, ROUNDS, 2)),
            dma((ROUNDS, 5)),
            dma((ROUNDS, 4)),
            dma((2,)),
            dma((2,)),
            dma((2,)),
            dma((3,)),
            dma((1,)),
            dma((1,)),
            dma((ROUNDS, per_round)),
            dma((CHIPS, experts)),
            pltpu.SemaphoreType.REGULAR((SPREAD,)),
        ],
        compiler_params=pltpu.CompilerParams(
            collective_id=0, has_side_effects=True, vmem_limit_bytes=67_043_328
        ),
        name="moe_input_grad",
    )(
        route_ids.reshape(1, tokens),
        gate_pre[0, 0, 0],
        up_pre[0, 0, 0],
        hid_grad[0, 0, 0],
        w_gate[0, 0],
        w_up[0, 0],
    )
    return out[None]


def solution(mesh):
    placed = (
        P(None, ("section", "expert"), None),
        P("section", None, "expert", None, None),
        P("section", None, "expert", None, None),
        P("section", None, "expert", None, None),
        P("section", "expert", None, None),
        P("section", "expert", None, None),
    )
    return jax.shard_map(
        local,
        mesh=mesh,
        in_specs=placed,
        out_specs=P(None, ("section", "expert"), None),
        check_vma=False,
    )
```

```python
import functools

import jax
import jax.numpy as jnp
from jax import lax
from jax.experimental import pallas as pl
from jax.experimental.pallas import tpu as pltpu
from jax.sharding import PartitionSpec as P

GRP = 8
CHIPS = 4
ROUNDS = 4
AHEAD = 4
GRID_X, GRID_Y = 4, 8
SPREAD = GRID_X // 2 + GRID_Y // 2 + 1
LANES = 128
MESH = pl.DeviceIdType.MESH


def kernel(
    sections, devices, cap,
    ids_ref, gate_ref, up_ref, hid_ref, wg_ref, wu_ref,
    out_ref,
    gate_in, up_in, hid_in, act, other, weight, acc, stage, msg, recv, ids_in, pick,
    act_recv, own_send, fwd_send, w_send, w_recv, w_local, in_local, id_send, id_recv, msg_send, msg_recv, told,
):
    experts = devices // GRP
    half = devices // 2
    per_round = half // ROUNDS
    rows = per_round * cap
    half_rows = half * cap
    feats = wg_ref.shape[0]
    blocks = 2 * feats // LANES

    s = lax.axis_index("section")
    p = lax.axis_index("expert")
    e = p // GRP
    c = (p % GRP) // 2
    k = p % 2
    turn = (e + 1) % ROUNDS

    def near(chip, core):
        return (s, e * GRP + chip * 2 + core)

    has_left, has_right = c > 0, c < CHIPS - 1
    sends_back, gets_back = s > 0, s < sections - 1
    x, y = p // (2 * GRID_Y), p // 2 % GRID_Y

    def at_grid(gx, gy):
        return (s, ((gx + GRID_X) % GRID_X * GRID_Y + (gy + GRID_Y) % GRID_Y) * 2 + k)

    barrier = pltpu.get_barrier_semaphore()

    def greet(device):
        pl.semaphore_signal(barrier, inc=1, device_id=device, device_id_type=MESH)

    @pl.when(gets_back)
    def _():
        greet((s + 1, p))

    @pl.when(sends_back)
    def _():
        greet(near(c, 1 - k))
        for gx, gy in ((x - 1, y), (x + 1, y), (x, y - 1), (x, y + 1)):
            greet(at_grid(gx, gy))

        @pl.when(has_left)
        def _():
            greet(near(c - 1, 1 - k))

        @pl.when(has_right)
        def _():
            greet(near(c + 1, 1 - k))

    def tell(step):
        if step < GRID_X // 2:
            devices_told = [at_grid(x - 1, y), at_grid(x + 1, y)]
        elif step < SPREAD - 1:
            devices_told = [at_grid(x, y - 1), at_grid(x, y + 1)]
        else:
            devices_told = [near(c, 1 - k)]
        for device in devices_told:
            pl.semaphore_signal(told.at[step], inc=1, device_id=device, device_id_type=MESH)

    def hear(step):
        pl.semaphore_wait(told.at[step], 1 if step == SPREAD - 1 else 2)

    w_rows = pl.ds(pl.multiple_of(k * feats, feats), feats)
    local_g = pltpu.make_async_copy(wg_ref, weight.at[0, w_rows], w_local.at[0])
    local_u = pltpu.make_async_copy(wu_ref, weight.at[1, w_rows], w_local.at[1])
    loads = [
        pltpu.make_async_copy(ref, dst, in_local.at[i])
        for i, (ref, dst) in enumerate(((gate_ref, gate_in), (up_ref, up_in), (hid_ref, hid_in)))
    ]

    def derive(start):
        at = pl.ds(pl.multiple_of(start, 8), rows)
        gate_val = gate_in[at, :].astype(jnp.float32)
        up_val = up_in[at, :].astype(jnp.float32)
        grad_val = hid_in[at, :].astype(jnp.float32)
        sigma = jax.nn.sigmoid(gate_val)
        part = grad_val * sigma
        gate_grad = part * up_val * (1.0 + gate_val * (1.0 - sigma))
        return gate_grad.astype(jnp.bfloat16), (part * gate_val).astype(jnp.bfloat16)

    def derive_round(r):
        chunk = (r + turn) % ROUNDS
        gate_grad, up_grad = derive(k * half_rows + chunk * rows)
        act[c, r, k, :, :LANES] = gate_grad
        act[c, r, k, :, LANES:] = up_grad
        gate_grad, up_grad = derive((1 - k) * half_rows + chunk * rows)
        other[r, :, :LANES] = gate_grad
        other[r, :, LANES:] = up_grad

    def remote(src, dst, send, recv_sem, device):
        return pltpu.make_async_remote_copy(
            src_ref=src, dst_ref=dst, send_sem=send, recv_sem=recv_sem,
            device_id=device, device_id_type=MESH,
        )

    def own_copies(r, chip, side):
        same = remote(
            act.at[c, r, k], act.at[c, r, k], own_send.at[r, 2 * side], act_recv.at[c, r, k], near(chip, k)
        )
        cross = remote(
            other.at[r], act.at[c, r, k], own_send.at[r, 2 * side + 1], act_recv.at[c, r, k], near(chip, 1 - k)
        )
        return same, cross

    def own_partner(r):
        return remote(
            other.at[r], act.at[c, r, k], own_send.at[r, 4], act_recv.at[c, r, k], near(c, 1 - k)
        )

    def forward(r, source, chip, slot):
        return remote(
            act.at[source, r], act.at[source, r], fwd_send.at[r, slot], act_recv.at[source, r, 0], near(chip, k)
        )

    def each_own(r, what):
        @pl.when(has_left)
        def _():
            for copy in own_copies(r, c - 1, 0):
                what(copy)

        @pl.when(has_right)
        def _():
            for copy in own_copies(r, c + 1, 1):
                what(copy)

        what(own_partner(r))

    def arrived(ref, sem):
        pltpu.make_async_copy(ref, ref, sem).wait()

    weight_g = remote(wg_ref, weight.at[0, w_rows], w_send.at[0], w_recv.at[0], near(c, 1 - k))
    weight_u = remote(wu_ref, weight.at[1, w_rows], w_send.at[1], w_recv.at[1], near(c, 1 - k))
    id_copy = remote(ids_ref, ids_in, id_send.at[0], id_recv.at[0], (s - 1, p))

    @pl.when(sends_back)
    def _():
        for load in loads:
            load.start()
        local_g.start()
        local_u.start()
        for load in loads:
            load.wait()
        derive_round(0)
        pl.semaphore_wait(
            barrier, 6 + has_left.astype(jnp.int32) + has_right.astype(jnp.int32)
        )
        each_own(0, lambda copy: copy.start())
        weight_g.start()
        weight_u.start()
        id_copy.start()
        tell(0)

        def early(r, carry):
            derive_round(r)

            @pl.when(r < AHEAD)
            def _():
                each_own(r, lambda copy: copy.start())

            return carry

        lax.fori_loop(1, ROUNDS, early, 0)
        stage[...] = jnp.zeros_like(stage)

    def back(r, i):
        owner = k * half + ((r + turn) % ROUNDS) * per_round + i
        return remote(
            msg.at[r, i], recv.at[c, e], msg_send.at[r, i], msg_recv.at[c, e], (s - 1, owner)
        )

    def relay(r):
        @pl.when((r > 0) & (r + AHEAD - 1 < ROUNDS))
        def _():
            each_own(r + AHEAD - 1, lambda copy: copy.start())

        @pl.when(has_left)
        def _():
            arrived(act.at[c - 1, r, 0], act_recv.at[c - 1, r, 0])
            arrived(act.at[c - 1, r, 1], act_recv.at[c - 1, r, 1])

            @pl.when(has_right)
            def _():
                forward(r, c - 1, c + 1, 0).start()

        @pl.when(has_right)
        def _():
            arrived(act.at[c + 1, r, 0], act_recv.at[c + 1, r, 0])
            arrived(act.at[c + 1, r, 1], act_recv.at[c + 1, r, 1])

            @pl.when(has_left)
            def _():
                forward(r, c + 1, c - 1, 1).start()

        for turn_of in range(2):
            @pl.when(r == turn_of)
            def _(step=2 * turn_of):
                hear(step)
                tell(step + 1)

        @pl.when(c >= 2)
        def _():
            arrived(act.at[c - 2, r], act_recv.at[c - 2, r, 0])

            @pl.when(has_right)
            def _():
                forward(r, c - 2, c + 1, 2).start()

        @pl.when(c < CHIPS - 2)
        def _():
            arrived(act.at[c + 2, r], act_recv.at[c + 2, r, 0])

            @pl.when(has_left)
            def _():
                forward(r, c + 2, c - 1, 3).start()

        for turn_of in range(2):
            @pl.when(r == turn_of)
            def _(step=2 * turn_of + 1):
                hear(step)
                tell(step + 1)

    def compute(r):
        arrived(act.at[c, r, 1 - k], act_recv.at[c, r, 1 - k])

        @pl.when(r == 0)
        def _():
            local_g.wait()
            local_u.wait()
            partner_rows = pl.ds(pl.multiple_of((1 - k) * feats, feats), feats)
            arrived(weight.at[0, partner_rows], w_recv.at[0])
            arrived(weight.at[1, partner_rows], w_recv.at[1])

        @pl.when(c == CHIPS - 1)
        def _():
            arrived(act.at[0, r], act_recv.at[0, r, 0])

        @pl.when(c == 0)
        def _():
            arrived(act.at[CHIPS - 1, r], act_recv.at[CHIPS - 1, r, 0])

        @pl.when(r == 0)
        def _():
            hear(4)
            tell(5)

        lhs = [
            jnp.concatenate(
                [act[chip, r, core, :, g * LANES:(g + 1) * LANES] for chip in range(CHIPS) for core in range(2)],
                axis=1,
            )
            for g in range(2)
        ]
        contract = (((1,), (1,)), ((), ()))
        for start in range(0, 2 * feats, 2 * LANES):
            size = min(2 * LANES, 2 * feats - start)
            total = None
            for g in range(2):
                term = lax.dot_general(
                    lhs[g], weight[g, start:start + size, :], contract, preferred_element_type=jnp.float32
                )
                total = term if total is None else total + term
            acc[:, start:start + size] = total

        @pl.when(r == 0)
        def _():
            hear(5)
            tell(6)

        for i in range(per_round):
            for n in range(blocks):
                stage[i % 2, n * cap:(n + 1) * cap, :] = acc[i * cap:(i + 1) * cap, n * LANES:(n + 1) * LANES]
            msg[r, i] = stage[i % 2].astype(jnp.bfloat16)

        @pl.when(r == 0)
        def _():
            hear(6)

        def send(i, carry):
            back(r, (i + 2 * c + e) % per_round).start()
            return carry

        lax.fori_loop(0, per_round, send, 0)

    @pl.when(sends_back)
    def _():
        def relay_step(r, carry):
            relay(r)
            return carry

        def compute_step(r, carry):
            compute(r)
            return carry

        lax.fori_loop(0, ROUNDS, relay_step, 0)
        lax.fori_loop(0, ROUNDS, compute_step, 0)

    deep = recv.shape[2]
    width = experts * deep
    tokens = ids_ref.shape[1]

    @pl.when(gets_back)
    def _():
        arrived(ids_in, id_recv.at[0])
        row = jnp.broadcast_to(ids_in[...], (tokens, tokens))
        ti = lax.broadcasted_iota(jnp.int32, (tokens, tokens), 0)
        tj = lax.broadcasted_iota(jnp.int32, (tokens, tokens), 1)
        expert = jnp.sum(jnp.where(ti == tj, row, 0), axis=1, keepdims=True)
        earlier = jnp.where((row == expert) & (tj < ti), 1, 0)
        place = jnp.sum(earlier, axis=1, keepdims=True) + expert * deep
        lane = lax.broadcasted_iota(jnp.int32, (tokens, width), 1) - place
        for n in range(blocks):
            pick[n * tokens:(n + 1) * tokens, :] = jnp.where(lane == n * cap, 1.0, 0.0).astype(jnp.bfloat16)

        for pair in range(0, CHIPS, 2):
            for chip in (pair, pair + 1):
                for expert_at in range(experts):
                    arrived(recv.at[chip, expert_at], msg_recv.at[chip, expert_at])

            rhs = jnp.concatenate(
                [recv[pair].reshape(width, LANES), recv[pair + 1].reshape(width, LANES)], axis=1
            )
            got = jnp.dot(pick[...], rhs, preferred_element_type=jnp.float32).astype(jnp.bfloat16)
            for j in range(2):
                for n in range(blocks):
                    at = ((pair + j) * blocks + n) * LANES
                    out_ref[:, at:at + LANES] = got[n * tokens:(n + 1) * tokens, j * LANES:(j + 1) * LANES]

    @pl.when(jnp.logical_not(gets_back))
    def _():
        out_ref[...] = jnp.zeros_like(out_ref)

    def drain(r, carry):
        each_own(r, lambda copy: copy.wait_send())

        @pl.when(has_left & has_right)
        def _():
            forward(r, c - 1, c + 1, 0).wait_send()
            forward(r, c + 1, c - 1, 1).wait_send()

        @pl.when((c >= 2) & has_right)
        def _():
            forward(r, c - 2, c + 1, 2).wait_send()

        @pl.when((c < CHIPS - 2) & has_left)
        def _():
            forward(r, c + 2, c - 1, 3).wait_send()

        def done(i, carry):
            back(r, i).wait_send()
            return carry

        lax.fori_loop(0, per_round, done, 0)
        return carry

    @pl.when(sends_back)
    def _():
        weight_g.wait_send()
        weight_u.wait_send()
        id_copy.wait_send()
        lax.fori_loop(0, ROUNDS, drain, 0)


def local(route_ids, gate_pre, up_pre, hid_grad, w_gate, w_up):
    sections, devices = lax.axis_size("section"), lax.axis_size("expert")
    slots, hidden = gate_pre.shape[3:]
    cap = slots // devices
    feats, width = w_gate.shape[2:]
    tokens = route_ids.shape[1]
    experts = devices // GRP
    per_round = devices // 2 // ROUNDS
    rows = per_round * cap
    blocks = 2 * feats // LANES
    deep = -(-blocks * cap // 16) * 16
    vmem = pl.BlockSpec(memory_space=pltpu.VMEM)
    hbm = pl.BlockSpec(memory_space=pl.ANY)
    bf16 = jnp.bfloat16
    dma = pltpu.SemaphoreType.DMA
    out = pl.pallas_call(
        functools.partial(kernel, sections, devices, cap),
        out_shape=jax.ShapeDtypeStruct((tokens, GRP * feats), bf16),
        in_specs=[vmem, hbm, hbm, hbm, hbm, hbm],
        out_specs=vmem,
        scratch_shapes=[
            pltpu.VMEM((slots, hidden), bf16),
            pltpu.VMEM((slots, hidden), bf16),
            pltpu.VMEM((slots, hidden), bf16),
            pltpu.VMEM((CHIPS, ROUNDS, 2, rows, 2 * hidden), bf16),
            pltpu.VMEM((ROUNDS, rows, 2 * hidden), bf16),
            pltpu.VMEM((2, 2 * feats, width), bf16),
            pltpu.VMEM((rows, 2 * feats), jnp.float32),
            pltpu.VMEM((2, deep, LANES), jnp.float32),
            pltpu.VMEM((ROUNDS, per_round, deep, LANES), bf16),
            pltpu.VMEM((CHIPS, experts, deep, LANES), bf16),
            pltpu.VMEM((1, tokens), jnp.int32),
            pltpu.VMEM((blocks * tokens, experts * deep), bf16),
            dma((CHIPS, ROUNDS, 2)),
            dma((ROUNDS, 5)),
            dma((ROUNDS, 4)),
            dma((2,)),
            dma((2,)),
            dma((2,)),
            dma((3,)),
            dma((1,)),
            dma((1,)),
            dma((ROUNDS, per_round)),
            dma((CHIPS, experts)),
            pltpu.SemaphoreType.REGULAR((SPREAD,)),
        ],
        compiler_params=pltpu.CompilerParams(
            collective_id=0, has_side_effects=True, vmem_limit_bytes=67_043_328
        ),
        name="moe_input_grad",
    )(
        route_ids.reshape(1, tokens),
        gate_pre[0, 0, 0],
        up_pre[0, 0, 0],
        hid_grad[0, 0, 0],
        w_gate[0, 0],
        w_up[0, 0],
    )
    return out[None]


def solution(mesh):
    placed = (
        P(None, ("section", "expert"), None),
        P("section", None, "expert", None, None),
        P("section", None, "expert", None, None),
        P("section", None, "expert", None, None),
        P("section", "expert", None, None),
        P("section", "expert", None, None),
    )
    return jax.shard_map(
        local,
        mesh=mesh,
        in_specs=placed,
        out_specs=P(None, ("section", "expert"), None),
        check_vma=False,
    )
```
